32 devices in a mesh: groups: 2 (over y), expert: 8 (over z, x), head: 2 (over core).
Axes of the slice: x: 2, y: 2, z: 4, core: 2. Of those that a mesh axis runs over, the one named last changes fastest.
Arguments:
- moe_in: bfloat16 [128, 7168], P(('groups', 'expert'), 'head'), parts along dimension 0, may hold values from -6 to 6
- routes: int32 [128, 2], P(('groups', 'expert')), parts along dimension 0, may hold values from 0 to 7, all different within a row; in each aligned block of 8 rows (0 to 7, 8 to 15, ...) at most 2 rows name the same one
- gate_weights: float32 [128, 2], P(('groups', 'expert')), parts along dimension 0, may hold values from 0.1 to 1
- w_gate: bfloat16 [7168, 16384], P('head', 'expert'), may hold values from -0.0625 to 0.0625
- w_up: bfloat16 [7168, 16384], P('head', 'expert'), may hold values from -0.0625 to 0.0625
- w_down: bfloat16 [16384, 7168], P('expert', 'head'), may hold values from -0.125 to 0.125
Outputs:
- moe_out: bfloat16 [128, 7168], P(('groups', 'expert'), 'head'), parts along dimension 0
The draws below stay inside these ranges and needn't reach their ends.
There are 2 independent parts, one for each index of `groups`. The reference program is written for one: setup_inputs(seed, part) draws one part's arguments, and reference() takes and returns one part's arrays. A program takes and returns all parts, laid end to end along the dimension named above; an argument that names none is the same for every part. Nothing has to cross between parts.
Inputs may be any that keep to these rules, and one draw needn't show every extreme that they name: `routes`: each row names 2 different experts; among the 8 rows of one device no expert is named more than 2 times, a bound that some block reaches.
All inputs are finite; a program needn't handle non-finite values.
Results may differ from the reference program's by a relative error of at most 0.0058.
Values may be sent and summed in bfloat16 or wider, within the bound.
A program may use at most 128 MiB of HBM per device.

```python
import math
import jax
import jax.numpy as jnp
import numpy as np
from jax import lax

D = 7168
FF = 2048
FLIGHT = 8
TOPK = 2
RM = 8
CAP = 2
MOE_ROWS = 64
COLS = 16384
N_EXPERT = 8


def block_scale(key, extent, pieces, low, high):
    gain = 1.0
    for dim, parts in pieces:
        heights = jax.random.uniform(jax.random.fold_in(jax.random.fold_in(key, 6), dim), (parts,), jnp.float32, low / len(pieces), high / len(pieces))
        gain = gain * jnp.repeat(jnp.exp(heights), extent[dim] // parts).reshape((-1,) + (1,) * (len(extent) - 1 - dim))
    return gain


def shared_out(own_key, own, number, rows, amount, top, reach, lean):
    ranking = jax.random.permutation(own_key, amount)
    crowded, common = load_shares(amount, rows * top, reach, lean, True), load_shares(amount, rows * top, reach, lean, False)
    places = jnp.arange(amount)

    def named(lengths, turn):
        used = int((lengths > 0).sum())
        fixed = max(1, used // 4)
        moved = fixed + (places - fixed + turn * (used - fixed)) % max(1, amount - fixed)
        return jnp.zeros((amount,), jnp.int32).at[ranking[jnp.where(places < fixed, places, moved)]].set(jnp.asarray(lengths, jnp.int32))

    lengths = jnp.where(number % 4 == 0, named(crowded, number // 4), named(common, number - number // 4 - 1))
    mixed = jax.random.permutation(jax.random.fold_in(own, 3), amount)
    donor, sink = mixed[0:amount // 2 * 2:2], mixed[1:amount // 2 * 2:2]
    margin = jnp.minimum(lengths[donor] - 1, reach - lengths[sink]) // 2
    margin = jnp.where((donor == ranking[0]) | (sink == ranking[0]) | (lengths[sink] == 0), 0, jnp.maximum(margin, 0))
    moved = jax.random.randint(jax.random.fold_in(own, 4), (amount // 2,), 0, 1 << 20) % (margin + 1)
    lengths = lengths.at[donor].add(-moved).at[sink].add(moved)
    labels = jnp.searchsorted(jnp.cumsum(lengths), jnp.arange(rows * top), side="right").astype(jnp.int32)
    grid = labels.reshape(top, rows).T
    grid = grid[jax.random.permutation(jax.random.fold_in(own, 1), rows)]
    turn = jax.random.randint(jax.random.fold_in(own, 2), (rows, 1), 0, top)
    return jnp.take_along_axis(grid, (jnp.arange(top)[None, :] + turn) % top, axis=1)


def load_shares(number_of, total, limit, lean, full):
    portions = [(1 << 20) // math.isqrt(standing ** lean) + 1 for standing in range(1, number_of + 1)]
    largest = limit if full else min(limit, max(-(-total // number_of), total * portions[0] // sum(portions)))
    least = 1 if total - largest >= number_of - 1 else 0
    counts, rest = [largest] + [least] * (number_of - 1), total - largest - least * (number_of - 1)
    while rest > 0:
        candidates = [i for i in range(1, number_of) if counts[i] < largest] or [i for i in range(1, number_of) if counts[i] < limit]
        pool, remaining = sum([portions[i] for i in candidates]), rest
        for i in candidates:
            addition = min(limit - counts[i], max(1, remaining * portions[i] // pool), rest)
            counts[i] = counts[i] + addition
            rest = rest - addition
    return np.array(counts)


def noise(stream_key, extent, spread, bound, split=(), kind=jnp.bfloat16):
    array = spread * jax.random.normal(stream_key, extent, jnp.float32)
    if split:
        array = array * block_scale(stream_key, extent, split, -0.22, 0.18)
    return jnp.clip(array, -bound, bound).astype(kind)


def setup_inputs(seed: int = 0, part: int = 0) -> dict:
    seeds = jax.random.split(jax.random.key(seed), 7)
    part_keys = jax.random.split(jax.random.fold_in(seeds[6], part), 7)
    moe_in = noise(part_keys[0], (MOE_ROWS, D), 1.0, 6.0, ((0, 8), (1, 2)))
    routes_keys = jax.random.split(jax.random.fold_in(part_keys[1], 1), MOE_ROWS // RM)
    routes_turns = jax.random.permutation(jax.random.fold_in(part_keys[1], 3), MOE_ROWS // RM)
    routes = jax.vmap(lambda own, number: shared_out(jax.random.fold_in(part_keys[1], 2), own, number, RM, FLIGHT, TOPK, CAP, 2))(routes_keys, routes_turns).reshape((MOE_ROWS, TOPK))
    gate_weights = jnp.clip(0.1 + 0.9 * jax.random.uniform(part_keys[2], (MOE_ROWS, TOPK), jnp.float32) ** block_scale(part_keys[2], (MOE_ROWS, TOPK), ((0, 8),), -0.2, 0.2), 0.1, 1.0)
    w_gate = noise(seeds[3], (D, COLS), D ** -0.5, 0.0625, ((0, 2), (1, 8)))
    w_up = noise(seeds[4], (D, COLS), D ** -0.5, 0.0625, ((0, 2), (1, 8)))
    w_down = noise(seeds[5], (COLS, D), FF ** -0.5, 0.125, ((0, 8), (1, 2)))
    return {"moe_in": moe_in, "routes": routes, "gate_weights": gate_weights, "w_gate": w_gate, "w_up": w_up, "w_down": w_down}


def experts(moe_in, routes, gate_weights, w_gate, w_up, w_down):
    split_count = N_EXPERT // FLIGHT
    slice_width = FF // split_count
    row_bound = N_EXPERT * CAP

    def one_expert(carry, expert):
        matched = routes == expert
        chosen = jnp.any(matched, axis=1)
        gate_hit = jnp.sum(jnp.where(matched, gate_weights, 0.0), axis=1)
        sorting = jnp.argsort(jnp.where(chosen, 0, 1).astype(jnp.int32), stable=True)[:row_bound].astype(jnp.int32)
        picked = moe_in[sorting]
        gate_cols = lax.dynamic_slice_in_dim(w_gate, expert * FF, FF, 1)
        up_cols = lax.dynamic_slice_in_dim(w_up, expert * FF, FF, 1)
        gate_pre = jnp.dot(picked, gate_cols, preferred_element_type=jnp.float32)
        up_pre = jnp.dot(picked, up_cols, preferred_element_type=jnp.float32)
        hidden = (jax.nn.silu(gate_pre) * up_pre).astype(jnp.bfloat16)
        down_rows = lax.dynamic_slice_in_dim(w_down, expert * FF, FF, 0)
        slice_out = jnp.einsum(
            "rsh,shd->rsd",
            hidden.reshape(row_bound, split_count, slice_width).astype(jnp.float32),
            down_rows.reshape(split_count, slice_width, D).astype(jnp.float32),
        )
        rounded = lax.optimization_barrier(slice_out.astype(jnp.bfloat16))
        expert_out = jnp.sum(rounded.astype(jnp.float32), axis=1)
        contrib = expert_out * gate_hit[sorting][:, None]
        return carry.at[sorting].add(contrib), None

    start = jnp.zeros(moe_in.shape, jnp.float32)
    summed, unused = lax.scan(one_expert, start, jnp.arange(FLIGHT, dtype=jnp.int32))
    return summed.astype(jnp.bfloat16)


def reference(moe_in, routes, gate_weights, w_gate, w_up, w_down):
    return experts(moe_in, routes, gate_weights, w_gate, w_up, w_down)
```

```python
import functools

import jax
import jax.numpy as jnp
from jax import lax
from jax.experimental import pallas as pl
from jax.experimental.pallas import tpu as pltpu
from jax.sharding import PartitionSpec as P

FLIGHT = 8
CAP = 2
GATE_COLS = 1024
DOWN_COLS = 896
MESH = pl.DeviceIdType.MESH


def chunk_of(total, most):
    best = 128 if total % 128 == 0 else total
    for width in range(128, most + 1, 128):
        if total % width == 0:
            best = width
    return best


def each(count, body):
    if count <= 16:
        for i in range(1, count):
            body(i)
    else:
        lax.fori_loop(1, count, lambda i, c: (body(i), c)[1], 0)


def placing_of(routes, slots, copies):
    top, rows = routes.shape
    shape = (slots * copies, rows)
    line = lax.broadcasted_iota(jnp.int32, shape, 0)
    expert = line // (CAP * copies)
    slot = (line % CAP).astype(jnp.float32)
    hits = [(routes[k : k + 1, :] == expert).astype(jnp.float32) for k in range(top)]
    chosen = sum(hits[1:], hits[0])
    r = lax.broadcasted_iota(jnp.int32, (rows, rows), 0)
    c = lax.broadcasted_iota(jnp.int32, (rows, rows), 1)
    before = jnp.dot(chosen, (r < c).astype(jnp.float32), preferred_element_type=jnp.float32)
    placing = chosen * (before == slot).astype(jnp.float32)
    return placing, hits


def kernel(
    n, copies, cf, cd,
    routes_h, weights_h, rows_h, gate_h, up_h, down_h, out_ref,
    routes_v, weights_v, rows_v, gate_v, up_v, down_v,
    packed, arrived, merged, mine, theirs, hidden, outbox, returned,
    small_sem, weight_sem, send_sem, recv_sem, self_sem,
    pair_send, pair_recv, back_send, back_recv, back_self,
):
    me = lax.axis_index("expert")
    partner = 1 - lax.axis_index("head")
    width = merged.shape[1]
    ff = gate_v.shape[1]
    nf, nd = ff // cf, width // cd

    small = [
        pltpu.make_async_copy(s, d, small_sem.at[i])
        for i, (s, d) in enumerate([(routes_h, routes_v), (weights_h, weights_v), (rows_h, rows_v)])
    ]
    for copy in small:
        copy.start()

    barrier = pltpu.get_barrier_semaphore()

    def greet(i):
        pl.semaphore_signal(
            barrier, inc=1, device_id={"expert": lax.rem(me + i, n)}, device_id_type=MESH
        )

    each(n, greet)
    pl.semaphore_signal(barrier, inc=1, device_id={"head": partner}, device_id_type=MESH)

    gates, ups, downs = [], [], []
    for j in range(nf):
        cols = pl.ds(j * cf, cf)
        gates.append(pltpu.make_async_copy(gate_h.at[:, cols], gate_v.at[:, cols], weight_sem.at[2 * j]))
        ups.append(pltpu.make_async_copy(up_h.at[:, cols], up_v.at[:, cols], weight_sem.at[2 * j + 1]))
        gates[-1].start()
        ups[-1].start()
    for j in range(nd):
        cols = pl.ds(j * cd, cd)
        downs.append(pltpu.make_async_copy(down_h.at[:, cols], down_v.at[:, cols], weight_sem.at[2 * nf + j]))
        downs[-1].start()

    for copy in small:
        copy.wait()
    placing, hits = placing_of(routes_v[...], FLIGHT * CAP, 1)
    picked = jnp.dot(
        placing.astype(jnp.bfloat16), rows_v[...], preferred_element_type=jnp.float32
    )
    for f in range(FLIGHT):
        packed[f] = picked[f * CAP : (f + 1) * CAP].astype(jnp.bfloat16)
    pl.semaphore_wait(barrier, n)

    def dispatch(i):
        peer = lax.rem(me + i, n)
        pltpu.make_async_remote_copy(
            src_ref=packed.at[peer // copies], dst_ref=arrived.at[me],
            send_sem=send_sem, recv_sem=recv_sem,
            device_id={"expert": peer}, device_id_type=MESH,
        ).start()

    each(n, dispatch)
    own = pltpu.make_async_copy(packed.at[me // copies], arrived.at[me], self_sem)
    own.start()

    if copies == 1:
        wide = placing
    else:
        wide, hits = placing_of(routes_v[...], FLIGHT * CAP, copies)
    weight = sum(
        [hits[k] * weights_v[k : k + 1, :] for k in range(1, len(hits))],
        hits[0] * weights_v[0:1, :],
    )
    spread = (wide * weight).T

    own.wait()
    others = arrived.at[pl.ds(0, n - 1)]
    pltpu.make_async_copy(others, others, recv_sem).wait()
    for s in range(n):
        if s % 8 == 0:
            group = [arrived[t].astype(jnp.float32) for t in range(s, min(s + 8, n))]
            merged[s * CAP : (s + len(group)) * CAP, :] = jnp.concatenate(group, axis=0).astype(
                jnp.bfloat16
            )

    pairs = []

    def activate(j):
        pairs[j].wait_recv()
        gate = mine[j, 0] + theirs[j, 0]
        up = mine[j, 1] + theirs[j, 1]
        hidden[:, pl.ds(j * cf, cf)] = (gate / (1.0 + jnp.exp(-gate)) * up).astype(jnp.bfloat16)

    for j in range(nf):
        cols = pl.ds(j * cf, cf)
        gates[j].wait()
        ups[j].wait()
        mine[j, 0] = jnp.dot(merged[...], gate_v[:, cols], preferred_element_type=jnp.float32)
        mine[j, 1] = jnp.dot(merged[...], up_v[:, cols], preferred_element_type=jnp.float32)
        pairs.append(
            pltpu.make_async_remote_copy(
                src_ref=mine.at[j], dst_ref=theirs.at[j],
                send_sem=pair_send.at[j], recv_sem=pair_recv.at[j],
                device_id={"head": partner}, device_id_type=MESH,
            )
        )
        pairs[-1].start()
        if j >= 1:
            activate(j - 1)

    activate(nf - 1)

    for j in range(nd):
        cols = pl.ds(j * cd, cd)
        downs[j].wait()
        part = jnp.dot(hidden[...], down_v[:, cols], preferred_element_type=jnp.float32)
        for s in range(n):
            outbox[j, s] = part[s * CAP : (s + 1) * CAP].astype(jnp.bfloat16)

        def give(i, j=j):
            peer = lax.rem(me + i, n)
            pltpu.make_async_remote_copy(
                src_ref=outbox.at[j, peer], dst_ref=returned.at[j, me],
                send_sem=back_send, recv_sem=back_recv.at[j],
                device_id={"expert": peer}, device_id_type=MESH,
            ).start()

        each(n, give)
        pltpu.make_async_copy(outbox.at[j, me], returned.at[j, me], back_self.at[j]).start()

    for j in range(nd):
        pltpu.make_async_copy(outbox.at[j, me], returned.at[j, me], back_self.at[j]).wait()
        others_j = returned.at[j, pl.ds(0, n - 1)]
        pltpu.make_async_copy(others_j, others_j, back_recv.at[j]).wait()
        total = None
        for s in range(0, n, 8):
            e = min(s + 8, n)
            rows = jnp.concatenate([returned[j, t].astype(jnp.float32) for t in range(s, e)], axis=0)
            term = jnp.dot(
                spread[:, s * CAP : e * CAP], rows,
                precision=lax.Precision.HIGHEST, preferred_element_type=jnp.float32,
            )
            total = term if total is None else total + term
        out_ref[:, pl.ds(j * cd, cd)] = total.astype(out_ref.dtype)

    pltpu.make_async_copy(others, others, send_sem).wait()
    for j in range(nf):
        pairs[j].wait_send()
    for j in range(nd):
        others_j = outbox.at[j, pl.ds(0, n - 1)]
        pltpu.make_async_copy(others_j, others_j, back_send).wait()


def per_device(moe_in, routes, gate_weights, w_gate, w_up, w_down):
    n = lax.axis_size("expert")
    copies = n // FLIGHT
    routes, gate_weights = routes.T, gate_weights.T
    rows, width = moe_in.shape
    ff = w_gate.shape[1]
    count = n * CAP
    cf, cd = chunk_of(ff, GATE_COLS), chunk_of(width, DOWN_COLS)
    nf, nd = ff // cf, width // cd
    bf16, f32 = jnp.bfloat16, jnp.float32
    anywhere = pl.BlockSpec(memory_space=pltpu.HBM)
    dma = pltpu.SemaphoreType.DMA
    return pl.pallas_call(
        functools.partial(kernel, n, copies, cf, cd),
        out_shape=jax.ShapeDtypeStruct((rows, width), bf16),
        in_specs=[anywhere] * 6,
        out_specs=pl.BlockSpec(memory_space=pltpu.VMEM),
        scratch_shapes=[
            pltpu.VMEM(routes.shape, routes.dtype),
            pltpu.VMEM(gate_weights.shape, gate_weights.dtype),
            pltpu.VMEM(moe_in.shape, moe_in.dtype),
            pltpu.VMEM(w_gate.shape, w_gate.dtype),
            pltpu.VMEM(w_up.shape, w_up.dtype),
            pltpu.VMEM(w_down.shape, w_down.dtype),
            pltpu.VMEM((FLIGHT, CAP, width), bf16),
            pltpu.VMEM((n, CAP, width), bf16),
            pltpu.VMEM((count, width), bf16),
            pltpu.VMEM((nf, 2, count, cf), f32),
            pltpu.VMEM((nf, 2, count, cf), f32),
            pltpu.VMEM((count, ff), bf16),
            pltpu.VMEM((nd, n, CAP, cd), bf16),
            pltpu.VMEM((nd, n, CAP, cd), bf16),
            dma((3,)), dma((2 * nf + nd,)), dma, dma, dma,
            dma((nf,)), dma((nf,)), dma, dma((nd,)), dma((nd,)),
        ],
        compiler_params=pltpu.CompilerParams(
            vmem_limit_bytes=50 << 20, collective_id=0, has_side_effects=True),
    )(*[pltpu.with_memory_space_constraint(v, pltpu.HBM) for v in (routes, gate_weights, moe_in)], w_gate, w_up, w_down)


def solution(mesh):
    in_specs = (
        P(("groups", "expert"), "head"),
        P(("groups", "expert"), None),
        P(("groups", "expert"), None),
        P("head", "expert"),
        P("head", "expert"),
        P("expert", "head"),
    )
    out_specs = P(("groups", "expert"), "head")
    return jax.shard_map(
        per_device, mesh=mesh, in_specs=in_specs, out_specs=out_specs, check_vma=False
    )
```

```python
import functools

import jax
import jax.numpy as jnp
from jax import lax
from jax.experimental import pallas as pl
from jax.experimental.pallas import tpu as pltpu
from jax.sharding import PartitionSpec as P

FLIGHT = 8
CAP = 2
FEATURES = 1792
GATE_COLS = 1024
DOWN_COLS = 1024
EARLY = 2
MESH = pl.DeviceIdType.MESH


def cuts_of(total, most):
    return [(at, min(most, total - at)) for at in range(0, total, most)]


def each(count, body):
    if count <= 16:
        for i in sorted(range(1, count), key=lambda i: abs(2 * i - count)):
            body(i)
    else:
        lax.fori_loop(1, count, lambda i, c: (body(i), c)[1], 0)


def placing_of(routes, slots, copies):
    top, rows = routes.shape
    shape = (slots * copies, rows)
    line = lax.broadcasted_iota(jnp.int32, shape, 0)
    expert = line // (CAP * copies)
    slot = (line % CAP).astype(jnp.float32)
    hits = [(routes[k : k + 1, :] == expert).astype(jnp.float32) for k in range(top)]
    chosen = sum(hits[1:], hits[0])
    r = lax.broadcasted_iota(jnp.int32, (rows, rows), 0)
    c = lax.broadcasted_iota(jnp.int32, (rows, rows), 1)
    before = jnp.dot(chosen, (r < c).astype(jnp.float32), preferred_element_type=jnp.float32)
    placing = chosen * (before == slot).astype(jnp.float32)
    return placing, hits


def kernel(
    n, copies, kcuts, fcuts, dcuts,
    routes_h, weights_h, rows_h, gate_h, up_h, down_h, out_ref,
    routes_v, weights_v, rows_v, gate_v, up_v, down_v,
    packed, arrived, merged, mine, theirs, hidden, begun, outbox, returned,
    small_sem, weight_sem, send_sem, recv_sem,
    pair_send, pair_recv, back_send, back_recv,
):
    me = lax.axis_index("expert")
    partner = 1 - lax.axis_index("head")
    nk, nf, nd = len(kcuts), len(fcuts), len(dcuts)

    small = [
        pltpu.make_async_copy(s, d, small_sem.at[i])
        for i, (s, d) in enumerate([(routes_h, routes_v), (weights_h, weights_v), (rows_h, rows_v)])
    ]
    for copy in small:
        copy.start()

    streams = []

    def stream(source, target, lines, cols):
        where = (pl.ds(*lines), pl.ds(*cols))
        streams.append(
            pltpu.make_async_copy(source.at[where], target.at[where], weight_sem.at[len(streams)])
        )
        return streams[-1]

    whole = (0, gate_v.shape[1])
    firsts = [
        [stream(gate_h, gate_v, lines, whole), stream(up_h, up_v, lines, whole)]
        for lines in kcuts[:-1]
    ]
    lasts = [
        [stream(gate_h, gate_v, kcuts[-1], cols), stream(up_h, up_v, kcuts[-1], cols)]
        for cols in fcuts
    ]
    downs = [stream(down_h, down_v, (0, down_v.shape[0]), cols) for cols in dcuts]
    streams[0].start()

    barrier = pltpu.get_barrier_semaphore()

    def greet(i):
        pl.semaphore_signal(
            barrier, inc=1, device_id={"expert": lax.rem(me + i, n)}, device_id_type=MESH
        )

    each(n, greet)
    pl.semaphore_signal(barrier, inc=1, device_id={"head": partner}, device_id_type=MESH)
    for copy in streams[1:]:
        copy.start()

    for copy in small:
        copy.wait()
    placing, hits = placing_of(routes_v[...], FLIGHT * CAP, 1)
    picked = jnp.dot(
        placing.astype(jnp.bfloat16), rows_v[...], preferred_element_type=jnp.float32
    )
    for f in range(FLIGHT):
        packed[f] = picked[f * CAP : (f + 1) * CAP].astype(jnp.bfloat16)
    pl.semaphore_wait(barrier, n)

    for k in range(nk):
        cols = pl.ds(*kcuts[k])

        def dispatch(i, k=k, cols=cols):
            peer = lax.rem(me + i, n)
            pltpu.make_async_remote_copy(
                src_ref=packed.at[peer // copies, :, cols], dst_ref=arrived.at[me, :, cols],
                send_sem=send_sem, recv_sem=recv_sem.at[k],
                device_id={"expert": peer}, device_id_type=MESH,
            ).start()

        each(n, dispatch)
    arrived[me] = packed[me // copies]

    if copies == 1:
        wide = placing
    else:
        wide, hits = placing_of(routes_v[...], FLIGHT * CAP, copies)
    weight = sum(
        [hits[k] * weights_v[k : k + 1, :] for k in range(1, len(hits))],
        hits[0] * weights_v[0:1, :],
    )
    spread = (wide * weight).T

    def gather(k):
        cols = pl.ds(*kcuts[k])
        others = arrived.at[pl.ds(0, n - 1), :, cols]
        pltpu.make_async_copy(others, others, recv_sem.at[k]).wait()
        for s in range(0, n, 8):
            group = [arrived[t, :, cols].astype(jnp.float32) for t in range(s, min(s + 8, n))]
            merged[s * CAP : (s + len(group)) * CAP, cols] = jnp.concatenate(
                group, axis=0
            ).astype(jnp.bfloat16)

    def product(k, weights, cols):
        lines = pl.ds(*kcuts[k])
        return jnp.dot(
            merged[:, lines], weights[lines, pl.ds(*cols)], preferred_element_type=jnp.float32
        )

    pairs = [
        pltpu.make_async_remote_copy(
            src_ref=mine.at[j], dst_ref=theirs.at[j],
            send_sem=pair_send.at[j], recv_sem=pair_recv.at[j],
            device_id={"head": partner}, device_id_type=MESH,
        )
        for j in range(nf)
    ]

    def activate(j):
        pairs[j].wait_recv()
        gate = mine[j, 0] + theirs[j, 0]
        up = mine[j, 1] + theirs[j, 1]
        hidden[:, pl.ds(*fcuts[j])] = (gate / (1.0 + jnp.exp(-gate)) * up).astype(jnp.bfloat16)

    for k in range(nk - 1):
        gather(k)
        for part, weights in enumerate([gate_v, up_v]):
            firsts[k][part].wait()
            for j in range(nf):
                term = product(k, weights, fcuts[j])
                mine[j, part] = term if k == 0 else mine[j, part] + term
    gather(nk - 1)
    for j in range(nf):
        for part, weights in enumerate([gate_v, up_v]):
            lasts[j][part].wait()
            term = product(nk - 1, weights, fcuts[j])
            mine[j, part] = term if nk == 1 else mine[j, part] + term
        pairs[j].start()
        if j >= 1:
            activate(j - 1)

    head = fcuts[-1][0]
    early = EARLY if head else 0
    for j in range(early):
        downs[j].wait()
        cols = pl.ds(*dcuts[j])
        begun[:, cols] = jnp.dot(
            hidden[:, :head], down_v[:head, cols], preferred_element_type=jnp.float32
        )
    activate(nf - 1)

    for j in range(nd):
        cols = pl.ds(*dcuts[j])
        if j < early:
            part = begun[:, cols] + jnp.dot(
                hidden[:, head:], down_v[head:, cols], preferred_element_type=jnp.float32
            )
        else:
            downs[j].wait()
            part = jnp.dot(hidden[...], down_v[:, cols], preferred_element_type=jnp.float32)
        for s in range(n):
            outbox[s, :, cols] = part[s * CAP : (s + 1) * CAP].astype(jnp.bfloat16)

        def give(i, j=j, cols=cols):
            peer = lax.rem(me + i, n)
            pltpu.make_async_remote_copy(
                src_ref=outbox.at[peer, :, cols], dst_ref=returned.at[me, :, cols],
                send_sem=back_send, recv_sem=back_recv.at[j],
                device_id={"expert": peer}, device_id_type=MESH,
            ).start()

        each(n, give)
    returned[me] = outbox[me]

    for j in range(nd):
        cols = pl.ds(*dcuts[j])
        others = returned.at[pl.ds(0, n - 1), :, cols]
        pltpu.make_async_copy(others, others, back_recv.at[j]).wait()
        total = None
        for s in range(0, n, 8):
            e = min(s + 8, n)
            rows = jnp.concatenate(
                [returned[t, :, cols].astype(jnp.float32) for t in range(s, e)], axis=0
            )
            term = jnp.dot(
                spread[:, s * CAP : e * CAP], rows,
                precision=lax.Precision.HIGHEST, preferred_element_type=jnp.float32,
            )
            total = term if total is None else total + term
        out_ref[:, cols] = total.astype(out_ref.dtype)

    for ref, sem in [(arrived, send_sem), (outbox, back_send)]:
        others = ref.at[pl.ds(0, n - 1)]
        pltpu.make_async_copy(others, others, sem).wait()
    for j in range(nf):
        pairs[j].wait_send()


def per_device(moe_in, routes, gate_weights, w_gate, w_up, w_down):
    n = lax.axis_size("expert")
    copies = n // FLIGHT
    routes, gate_weights = routes.T, gate_weights.T
    rows, width = moe_in.shape
    ff = w_gate.shape[1]
    count = n * CAP
    kcuts, fcuts, dcuts = cuts_of(width, FEATURES), cuts_of(ff, GATE_COLS), cuts_of(width, DOWN_COLS)
    nk, nf, nd = len(kcuts), len(fcuts), len(dcuts)
    bf16, f32 = jnp.bfloat16, jnp.float32
    anywhere = pl.BlockSpec(memory_space=pltpu.HBM)
    dma = pltpu.SemaphoreType.DMA
    return pl.pallas_call(
        functools.partial(kernel, n, copies, kcuts, fcuts, dcuts),
        out_shape=jax.ShapeDtypeStruct((rows, width), bf16),
        in_specs=[anywhere] * 6,
        out_specs=pl.BlockSpec(memory_space=pltpu.VMEM),
        scratch_shapes=[
            pltpu.VMEM(routes.shape, routes.dtype),
            pltpu.VMEM(gate_weights.shape, gate_weights.dtype),
            pltpu.VMEM(moe_in.shape, moe_in.dtype),
            pltpu.VMEM(w_gate.shape, w_gate.dtype),
            pltpu.VMEM(w_up.shape, w_up.dtype),
            pltpu.VMEM(w_down.shape, w_down.dtype),
            pltpu.VMEM((FLIGHT, CAP, width), bf16),
            pltpu.VMEM((n, CAP, width), bf16),
            pltpu.VMEM((count, width), bf16),
            pltpu.VMEM((nf, 2, count, fcuts[0][1]), f32),
            pltpu.VMEM((nf, 2, count, fcuts[0][1]), f32),
            pltpu.VMEM((count, ff), bf16),
            pltpu.VMEM((count, width), f32),
            pltpu.VMEM((n, CAP, width), bf16),
            pltpu.VMEM((n, CAP, width), bf16),
            dma((3,)), dma((2 * (nk - 1) + 2 * nf + nd,)), dma, dma((nk,)),
            dma((nf,)), dma((nf,)), dma, dma((nd,)),
        ],
        compiler_params=pltpu.CompilerParams(
            vmem_limit_bytes=50 << 20, collective_id=0, has_side_effects=True),
    )(*[pltpu.with_memory_space_constraint(v, pltpu.HBM) for v in (routes, gate_weights, moe_in)], w_gate, w_up, w_down)


def solution(mesh):
    in_specs = (
        P(("groups", "expert"), "head"),
        P(("groups", "expert"), None),
        P(("groups", "expert"), None),
        P("head", "expert"),
        P("head", "expert"),
        P("expert", "head"),
    )
    out_specs = P(("groups", "expert"), "head")
    return jax.shard_map(
        per_device, mesh=mesh, in_specs=in_specs, out_specs=out_specs, check_vma=False
    )
```

```python
import functools

import jax
import jax.numpy as jnp
from jax import lax
from jax.experimental import pallas as pl
from jax.experimental.pallas import tpu as pltpu
from jax.sharding import PartitionSpec as P

FLIGHT = 8
CAP = 2
FEATURES = (1792,)
GATE_COLS = (1024,)
DOWN_COLS = (1024,)
EARLY = 2
MESH = pl.DeviceIdType.MESH


def cuts_of(total, sizes):
    cuts, at = [], 0
    while at < total:
        size = min(sizes[min(len(cuts), len(sizes) - 1)], total - at)
        cuts.append((at, size))
        at += size
    return cuts


def each(me, n, body, far=True, near=True):
    half = n // 2
    if n <= 16 and n & (n - 1) == 0:
        flips, bit = {}, 1
        while bit < n:
            flips[bit] = bit - 2 * bit * (me // bit % 2)
            bit *= 2
        for i in range(n - 1, 0, -1):
            if far if i >= half else near:
                body(me + sum(flip for bit, flip in flips.items() if i & bit))
    elif n <= 16:
        for i in range(1, n):
            if far if i >= half else near:
                body(lax.rem(me + i, n))
    else:
        low, high = 1 if near else half, n if far else half
        lax.fori_loop(low, high, lambda i, c: (body(lax.rem(me + i, n)), c)[1], 0)


def placing_of(routes, slots, copies):
    top, rows = routes.shape
    shape = (slots * copies, rows)
    line = lax.broadcasted_iota(jnp.int32, shape, 0)
    expert = line // (CAP * copies)
    slot = (line % CAP).astype(jnp.float32)
    hits = [(routes[k : k + 1, :] == expert).astype(jnp.float32) for k in range(top)]
    chosen = sum(hits[1:], hits[0])
    r = lax.broadcasted_iota(jnp.int32, (rows, rows), 0)
    c = lax.broadcasted_iota(jnp.int32, (rows, rows), 1)
    before = jnp.dot(chosen, (r < c).astype(jnp.float32), preferred_element_type=jnp.float32)
    placing = chosen * (before == slot).astype(jnp.float32)
    return placing, hits


def kernel(
    n, copies, kcuts, fcuts, dcuts,
    routes_h, weights_h, rows_h, gate_h, up_h, down_h, out_ref,
    routes_v, weights_v, rows_v, gate_v, up_v, down_v,
    packed, arrived, merged, mine, theirs, hidden, begun, outbox, returned,
    small_sem, weight_sem, send_sem, recv_sem,
    pair_send, pair_recv, back_send, back_recv,
):
    me = lax.axis_index("expert")
    partner = 1 - lax.axis_index("head")
    nk, nf, nd = len(kcuts), len(fcuts), len(dcuts)

    small = [
        pltpu.make_async_copy(s, d, small_sem.at[i])
        for i, (s, d) in enumerate([(routes_h, routes_v), (weights_h, weights_v), (rows_h, rows_v)])
    ]
    for copy in small:
        copy.start()

    streams = []

    def stream(source, target, lines, cols):
        where = (pl.ds(*lines), pl.ds(*cols))
        streams.append(
            pltpu.make_async_copy(source.at[where], target.at[where], weight_sem.at[len(streams)])
        )
        return streams[-1]

    whole = (0, gate_v.shape[1])
    firsts = [
        [stream(gate_h, gate_v, lines, whole), stream(up_h, up_v, lines, whole)]
        for lines in kcuts[:-1]
    ]
    lasts = [
        [stream(gate_h, gate_v, kcuts[-1], cols), stream(up_h, up_v, kcuts[-1], cols)]
        for cols in fcuts
    ]
    downs = [stream(down_h, down_v, (0, down_v.shape[0]), cols) for cols in dcuts]
    streams[0].start()

    barrier = pltpu.get_barrier_semaphore()

    def greet(peer):
        pl.semaphore_signal(barrier, inc=1, device_id={"expert": peer}, device_id_type=MESH)

    each(me, n, greet)
    pl.semaphore_signal(barrier, inc=1, device_id={"head": partner}, device_id_type=MESH)
    for copy in streams[1:]:
        copy.start()

    for copy in small:
        copy.wait()
    placing, hits = placing_of(routes_v[...], FLIGHT * CAP, 1)
    picked = jnp.dot(
        placing.astype(jnp.bfloat16), rows_v[...], preferred_element_type=jnp.float32
    )
    for f in range(FLIGHT):
        packed[f] = picked[f * CAP : (f + 1) * CAP].astype(jnp.bfloat16)
    pl.semaphore_wait(barrier, n)

    for far in [True, False]:
        for k in range(nk):
            cols = pl.ds(*kcuts[k])

            def dispatch(peer, k=k, cols=cols):
                pltpu.make_async_remote_copy(
                    src_ref=packed.at[peer // copies, :, cols], dst_ref=arrived.at[me, :, cols],
                    send_sem=send_sem, recv_sem=recv_sem.at[k],
                    device_id={"expert": peer}, device_id_type=MESH,
                ).start()

            each(me, n, dispatch, far=far, near=not far)
    arrived[me] = packed[me // copies]

    if copies == 1:
        wide = placing
    else:
        wide, hits = placing_of(routes_v[...], FLIGHT * CAP, copies)
    weight = sum(
        [hits[k] * weights_v[k : k + 1, :] for k in range(1, len(hits))],
        hits[0] * weights_v[0:1, :],
    )
    spread, thirds = (wide * weight).T, []
    for _ in range(3):
        thirds.append(spread.astype(jnp.bfloat16).astype(jnp.float32))
        spread = spread - thirds[-1]
    spread = jnp.concatenate(thirds, axis=0).astype(jnp.bfloat16)

    def gather(k):
        cols = pl.ds(*kcuts[k])
        others = arrived.at[pl.ds(0, n - 1), :, cols]
        pltpu.make_async_copy(others, others, recv_sem.at[k]).wait()
        merged[:, cols] = arrived[:, :, cols].reshape(n * CAP, kcuts[k][1])

    def product(k, weights, cols):
        lines = pl.ds(*kcuts[k])
        return jnp.dot(
            merged[:, lines], weights[lines, pl.ds(*cols)], preferred_element_type=jnp.float32
        )

    pairs = [
        pltpu.make_async_remote_copy(
            src_ref=mine.at[j], dst_ref=theirs.at[j],
            send_sem=pair_send.at[j], recv_sem=pair_recv.at[j],
            device_id={"head": partner}, device_id_type=MESH,
        )
        for j in range(nf)
    ]

    def activate(j):
        pairs[j].wait_recv()
        gate = mine[j, 0] + theirs[j, 0]
        up = mine[j, 1] + theirs[j, 1]
        hidden[:, pl.ds(*fcuts[j])] = (gate / (1.0 + jnp.exp(-gate)) * up).astype(jnp.bfloat16)

    for k in range(nk - 1):
        gather(k)
        for part, weights in enumerate([gate_v, up_v]):
            firsts[k][part].wait()
            term = product(k, weights, whole)
            for j in range(nf):
                piece = term[:, fcuts[j][0] : sum(fcuts[j])]
                mine[j, part] = piece if k == 0 else mine[j, part] + piece
    gather(nk - 1)
    for j in range(nf):
        for part, weights in enumerate([gate_v, up_v]):
            lasts[j][part].wait()
            term = product(nk - 1, weights, fcuts[j])
            mine[j, part] = term if nk == 1 else mine[j, part] + term
        pairs[j].start()
        if j >= 1:
            activate(j - 1)

    head = fcuts[-1][0]
    early = EARLY if head else 0
    for j in range(early):
        downs[j].wait()
        cols = pl.ds(*dcuts[j])
        begun[:, cols] = jnp.dot(
            hidden[:, :head], down_v[:head, cols], preferred_element_type=jnp.float32
        )
    activate(nf - 1)

    for j in range(nd):
        cols = pl.ds(*dcuts[j])
        if j < early:
            part = begun[:, cols] + jnp.dot(
                hidden[:, head:], down_v[head:, cols], preferred_element_type=jnp.float32
            )
        else:
            downs[j].wait()
            part = jnp.dot(hidden[...], down_v[:, cols], preferred_element_type=jnp.float32)
        outbox[:, :, cols] = part.astype(jnp.bfloat16).reshape(n, CAP, dcuts[j][1])

        def give(peer, j=j, cols=cols):
            pltpu.make_async_remote_copy(
                src_ref=outbox.at[peer, :, cols], dst_ref=returned.at[me, :, cols],
                send_sem=back_send, recv_sem=back_recv.at[j],
                device_id={"expert": peer}, device_id_type=MESH,
            ).start()

        each(me, n, give)
    returned[me] = outbox[me]

    for j in range(nd):
        cols = pl.ds(*dcuts[j])
        others = returned.at[pl.ds(0, n - 1), :, cols]
        pltpu.make_async_copy(others, others, back_recv.at[j]).wait()
        rows = returned[:, :, cols].reshape(n * CAP, dcuts[j][1])
        total = jnp.dot(spread, rows, preferred_element_type=jnp.float32)
        high, middle, low = jnp.split(total, 3, axis=0)
        out_ref[:, cols] = (high + (middle + low)).astype(out_ref.dtype)

    for ref, sem in [(arrived, send_sem), (outbox, back_send)]:
        others = ref.at[pl.ds(0, n - 1)]
        pltpu.make_async_copy(others, others, sem).wait()
    for j in range(nf):
        pairs[j].wait_send()


def per_device(moe_in, routes, gate_weights, w_gate, w_up, w_down):
    n = lax.axis_size("expert")
    copies = n // FLIGHT
    routes, gate_weights = routes.T, gate_weights.T
    rows, width = moe_in.shape
    ff = w_gate.shape[1]
    count = n * CAP
    kcuts, fcuts, dcuts = cuts_of(width, FEATURES), cuts_of(ff, GATE_COLS), cuts_of(width, DOWN_COLS)
    nk, nf, nd = len(kcuts), len(fcuts), len(dcuts)
    bf16, f32 = jnp.bfloat16, jnp.float32
    anywhere = pl.BlockSpec(memory_space=pltpu.HBM)
    dma = pltpu.SemaphoreType.DMA
    return pl.pallas_call(
        functools.partial(kernel, n, copies, kcuts, fcuts, dcuts),
        out_shape=jax.ShapeDtypeStruct((rows, width), bf16),
        in_specs=[anywhere] * 6,
        out_specs=pl.BlockSpec(memory_space=pltpu.VMEM),
        scratch_shapes=[
            pltpu.VMEM(routes.shape, routes.dtype),
            pltpu.VMEM(gate_weights.shape, gate_weights.dtype),
            pltpu.VMEM(moe_in.shape, moe_in.dtype),
            pltpu.VMEM(w_gate.shape, w_gate.dtype),
            pltpu.VMEM(w_up.shape, w_up.dtype),
            pltpu.VMEM(w_down.shape, w_down.dtype),
            pltpu.VMEM((FLIGHT, CAP, width), bf16),
            pltpu.VMEM((n, CAP, width), bf16),
            pltpu.VMEM((count, width), bf16),
            pltpu.VMEM((nf, 2, count, fcuts[0][1]), f32),
            pltpu.VMEM((nf, 2, count, fcuts[0][1]), f32),
            pltpu.VMEM((count, ff), bf16),
            pltpu.VMEM((count, width), f32),
            pltpu.VMEM((n, CAP, width), bf16),
            pltpu.VMEM((n, CAP, width), bf16),
            dma((3,)), dma((2 * (nk - 1) + 2 * nf + nd,)), dma, dma((nk,)),
            dma((nf,)), dma((nf,)), dma, dma((nd,)),
        ],
        compiler_params=pltpu.CompilerParams(
            vmem_limit_bytes=50 << 20, collective_id=0, has_side_effects=True),
    )(*[pltpu.with_memory_space_constraint(v, pltpu.HBM) for v in (routes, gate_weights, moe_in)], w_gate, w_up, w_down)


def solution(mesh):
    in_specs = (
        P(("groups", "expert"), "head"),
        P(("groups", "expert"), None),
        P(("groups", "expert"), None),
        P("head", "expert"),
        P("head", "expert"),
        P("expert", "head"),
    )
    out_specs = P(("groups", "expert"), "head")
    return jax.shard_map(
        per_device, mesh=mesh, in_specs=in_specs, out_specs=out_specs, check_vma=False
    )
```

```python
import functools

import jax
import jax.numpy as jnp
from jax import lax
from jax.experimental import pallas as pl
from jax.experimental.pallas import tpu as pltpu
from jax.sharding import PartitionSpec as P

FLIGHT = 8
CAP = 2
FEATURES = (2560, 1024)
GATE_COLS = (1024,)
DOWN_COLS = (1024, 768, 768, 512, 512)
EARLY = 2
MESH = pl.DeviceIdType.MESH


def cuts_of(total, sizes):
    cuts, at = [], 0
    while at < total:
        size = min(sizes[min(len(cuts), len(sizes) - 1)], total - at)
        cuts.append((at, size))
        at += size
    return cuts


def each(me, n, body, far=True, near=True):
    half = n // 2
    if n <= 16 and n & (n - 1) == 0:
        flips, bit = {}, 1
        while bit < n:
            flips[bit] = bit - 2 * bit * (me // bit % 2)
            bit *= 2
        for i in range(n - 1, 0, -1):
            if far if i >= half else near:
                body(me + sum(flip for bit, flip in flips.items() if i & bit))
    elif n <= 16:
        for i in range(1, n):
            if far if i >= half else near:
                body(lax.rem(me + i, n))
    else:
        low, high = 1 if near else half, n if far else half
        lax.fori_loop(low, high, lambda i, c: (body(lax.rem(me + i, n)), c)[1], 0)


def placing_of(routes, slots, copies):
    top, rows = routes.shape
    shape = (slots * copies, rows)
    line = lax.broadcasted_iota(jnp.int32, shape, 0)
    expert = line // (CAP * copies)
    slot = (line % CAP).astype(jnp.float32)
    hits = [(routes[k : k + 1, :] == expert).astype(jnp.float32) for k in range(top)]
    chosen = sum(hits[1:], hits[0])
    r = lax.broadcasted_iota(jnp.int32, (rows, rows), 0)
    c = lax.broadcasted_iota(jnp.int32, (rows, rows), 1)
    before = jnp.dot(chosen, (r < c).astype(jnp.float32), preferred_element_type=jnp.float32)
    placing = chosen * (before == slot).astype(jnp.float32)
    return placing, hits


def kernel(
    n, copies, kcuts, fcuts, dcuts,
    routes_h, weights_h, rows_h, gate_h, up_h, down_h, out_ref,
    routes_v, weights_v, rows_v, gate_v, up_v, down_v,
    packed, landed, merged, mine, theirs, hidden, begun, outbox,
    small_sem, weight_sem, send_sem, recv_sem,
    pair_send, pair_recv, back_recv,
):
    me = lax.axis_index("expert")
    partner = 1 - lax.axis_index("head")
    nk, nf, nd = len(kcuts), len(fcuts), len(dcuts)
    arrived, returned = landed.at[pl.ds(0, n)], landed.at[pl.ds(n, n)]

    small = [
        pltpu.make_async_copy(s, d, small_sem.at[i])
        for i, (s, d) in enumerate([(routes_h, routes_v), (weights_h, weights_v), (rows_h, rows_v)])
    ]
    for copy in small:
        copy.start()

    streams = []

    def stream(source, target, lines, cols):
        where = (pl.ds(*lines), pl.ds(*cols))
        streams.append(
            pltpu.make_async_copy(source.at[where], target.at[where], weight_sem.at[len(streams)])
        )
        return streams[-1]

    whole = (0, gate_v.shape[1])
    slabs = [
        [stream(gate_h, gate_v, lines, whole), stream(up_h, up_v, lines, whole)]
        for lines in kcuts
    ]
    downs = [stream(down_h, down_v, (0, down_v.shape[0]), cols) for cols in dcuts]
    streams[0].start()

    barrier = pltpu.get_barrier_semaphore()

    def greet(peer):
        pl.semaphore_signal(barrier, inc=1, device_id={"expert": peer}, device_id_type=MESH)

    each(me, n, greet)
    pl.semaphore_signal(barrier, inc=1, device_id={"head": partner}, device_id_type=MESH)
    for copy in streams[1:]:
        copy.start()

    for copy in small:
        copy.wait()
    placing, hits = placing_of(routes_v[...], FLIGHT * CAP, 1)
    picked = jnp.dot(
        placing.astype(jnp.bfloat16), rows_v[...], preferred_element_type=jnp.float32
    )
    for f in range(FLIGHT):
        packed[f] = picked[f * CAP : (f + 1) * CAP].astype(jnp.bfloat16)
    pl.semaphore_wait(barrier, n)

    for far in [True, False]:
        for k in range(nk):
            cols = pl.ds(*kcuts[k])

            def dispatch(peer, k=k, cols=cols):
                pltpu.make_async_remote_copy(
                    src_ref=packed.at[peer // copies, :, cols], dst_ref=arrived.at[me, :, cols],
                    send_sem=send_sem, recv_sem=recv_sem.at[k],
                    device_id={"expert": peer}, device_id_type=MESH,
                ).start()

            each(me, n, dispatch, far=far, near=not far)
    arrived[me] = packed[me // copies]

    if copies == 1:
        wide = placing
    else:
        wide, hits = placing_of(routes_v[...], FLIGHT * CAP, copies)
    weight = sum(
        [hits[k] * weights_v[k : k + 1, :] for k in range(1, len(hits))],
        hits[0] * weights_v[0:1, :],
    )
    spread, thirds = (wide * weight).T, []
    for _ in range(3):
        thirds.append(spread.astype(jnp.bfloat16).astype(jnp.float32))
        spread = spread - thirds[-1]
    spread = jnp.concatenate(thirds, axis=0).astype(jnp.bfloat16)

    def gather(k):
        cols = pl.ds(*kcuts[k])
        others = arrived.at[pl.ds(0, n - 1), :, cols]
        pltpu.make_async_copy(others, others, recv_sem.at[k]).wait()
        merged[:, cols] = arrived[:, :, cols].reshape(n * CAP, kcuts[k][1])

    def product(k, weights, cols):
        lines = pl.ds(*kcuts[k])
        return jnp.dot(
            merged[:, lines], weights[lines, pl.ds(*cols)], preferred_element_type=jnp.float32
        )

    pairs = [
        pltpu.make_async_remote_copy(
            src_ref=mine.at[j], dst_ref=theirs.at[j],
            send_sem=pair_send, recv_sem=pair_recv.at[j],
            device_id={"head": partner}, device_id_type=MESH,
        )
        for j in range(nf)
    ]

    def activate(j):
        pairs[j].wait_recv()
        gate = mine[j, 0] + theirs[j, 0]
        up = mine[j, 1] + theirs[j, 1]
        hidden[:, pl.ds(*fcuts[j])] = (gate / (1.0 + jnp.exp(-gate)) * up).astype(jnp.bfloat16)

    for k in range(nk - 1):
        gather(k)
        for part, weights in enumerate([gate_v, up_v]):
            slabs[k][part].wait()
            term = product(k, weights, whole)
            for j in range(nf):
                piece = term[:, fcuts[j][0] : sum(fcuts[j])]
                mine[j, part] = piece if k == 0 else mine[j, part] + piece
    gather(nk - 1)
    for part, weights in enumerate([gate_v, up_v]):
        slabs[nk - 1][part].wait()
        for j in range(nf):
            term = product(nk - 1, weights, fcuts[j])
            mine[j, part] = term if nk == 1 else mine[j, part] + term
            if part:
                pairs[j].start()
    for j in range(nf - 1):
        activate(j)

    head = fcuts[-1][0]
    early = EARLY if head else 0
    for j in range(early):
        downs[j].wait()
        cols = pl.ds(*dcuts[j])
        begun[:, cols] = jnp.dot(
            hidden[:, :head], down_v[:head, cols], preferred_element_type=jnp.float32
        )
    activate(nf - 1)

    def emit(j, part):
        cols = pl.ds(*dcuts[j])
        outbox[:, :, cols] = part.astype(jnp.bfloat16).reshape(n, CAP, dcuts[j][1])

        def give(peer):
            pltpu.make_async_remote_copy(
                src_ref=outbox.at[peer, :, cols], dst_ref=returned.at[me, :, cols],
                send_sem=send_sem, recv_sem=back_recv.at[j],
                device_id={"expert": peer}, device_id_type=MESH,
            ).start()

        each(me, n, give)

    ready = []
    for j in range(nd):
        cols = pl.ds(*dcuts[j])
        if j < early:
            part = begun[:, cols] + jnp.dot(
                hidden[:, head:], down_v[head:, cols], preferred_element_type=jnp.float32
            )
        else:
            downs[j].wait()
            part = jnp.dot(hidden[...], down_v[:, cols], preferred_element_type=jnp.float32)
        ready.append((j, part))
        while len(ready) > (1 if True else 0):
            emit(*ready.pop(0))
    for item in ready:
        emit(*item)
    returned[me] = outbox[me]

    for j in range(nd):
        cols = pl.ds(*dcuts[j])
        others = returned.at[pl.ds(0, n - 1), :, cols]
        pltpu.make_async_copy(others, others, back_recv.at[j]).wait()
        rows = returned[:, :, cols].reshape(n * CAP, dcuts[j][1])
        total = jnp.dot(spread, rows, preferred_element_type=jnp.float32)
        high, middle, low = jnp.split(total, 3, axis=0)
        out_ref[:, cols] = (high + (middle + low)).astype(out_ref.dtype)

    both = landed.at[pl.ds(0, 2 * n - 2)]
    pltpu.make_async_copy(both, both, send_sem).wait()
    pltpu.make_async_copy(mine, mine, pair_send).wait()


def per_device(moe_in, routes, gate_weights, w_gate, w_up, w_down):
    n = lax.axis_size("expert")
    copies = n // FLIGHT
    routes, gate_weights = routes.T, gate_weights.T
    rows, width = moe_in.shape
    ff = w_gate.shape[1]
    count = n * CAP
    kcuts, fcuts, dcuts = cuts_of(width, FEATURES), cuts_of(ff, GATE_COLS), cuts_of(width, DOWN_COLS)
    nk, nf, nd = len(kcuts), len(fcuts), len(dcuts)
    bf16, f32 = jnp.bfloat16, jnp.float32
    anywhere = pl.BlockSpec(memory_space=pltpu.HBM)
    dma = pltpu.SemaphoreType.DMA
    return pl.pallas_call(
        functools.partial(kernel, n, copies, kcuts, fcuts, dcuts),
        out_shape=jax.ShapeDtypeStruct((rows, width), bf16),
        in_specs=[anywhere] * 6,
        out_specs=pl.BlockSpec(memory_space=pltpu.VMEM),
        scratch_shapes=[
            pltpu.VMEM(routes.shape, routes.dtype),
            pltpu.VMEM(gate_weights.shape, gate_weights.dtype),
            pltpu.VMEM(moe_in.shape, moe_in.dtype),
            pltpu.VMEM(w_gate.shape, w_gate.dtype),
            pltpu.VMEM(w_up.shape, w_up.dtype),
            pltpu.VMEM(w_down.shape, w_down.dtype),
            pltpu.VMEM((FLIGHT, CAP, width), bf16),
            pltpu.VMEM((2 * n, CAP, width), bf16),
            pltpu.VMEM((count, width), bf16),
            pltpu.VMEM((nf, 2, count, fcuts[0][1]), f32),
            pltpu.VMEM((nf, 2, count, fcuts[0][1]), f32),
            pltpu.VMEM((count, ff), bf16),
            pltpu.VMEM((count, width), f32),
            pltpu.VMEM((n, CAP, width), bf16),
            dma((3,)), dma((2 * nk + nd,)), dma, dma((nk,)),
            dma, dma((nf,)), dma((nd,)),
        ],
        compiler_params=pltpu.CompilerParams(
            vmem_limit_bytes=50 << 20, collective_id=0, has_side_effects=True),
    )(*[pltpu.with_memory_space_constraint(v, pltpu.HBM) for v in (routes, gate_weights, moe_in)], w_gate, w_up, w_down)


def solution(mesh):
    in_specs = (
        P(("groups", "expert"), "head"),
        P(("groups", "expert"), None),
        P(("groups", "expert"), None),
        P("head", "expert"),
        P("head", "expert"),
        P("expert", "head"),
    )
    out_specs = P(("groups", "expert"), "head")
    return jax.shard_map(
        per_device, mesh=mesh, in_specs=in_specs, out_specs=out_specs, check_vma=False
    )
```

```python
import functools

import jax
import jax.numpy as jnp
from jax import lax
from jax.experimental import pallas as pl
from jax.experimental.pallas import tpu as pltpu
from jax.sharding import PartitionSpec as P

FLIGHT = 8
CAP = 2
FEATURES = (2560, 1024)
GATE_COLS = (1024,)
DOWN_COLS = (1024,)
EARLY = 2
MESH = pl.DeviceIdType.MESH


def cuts_of(total, sizes):
    cuts, at = [], 0
    while at < total:
        size = min(sizes[min(len(cuts), len(sizes) - 1)], total - at)
        cuts.append((at, size))
        at += size
    return cuts


def each(me, n, body, far=True, near=True):
    half = n // 2
    if n <= 16 and n & (n - 1) == 0:
        flips, bit = {}, 1
        while bit < n:
            flips[bit] = bit - 2 * bit * (me // bit % 2)
            bit *= 2
        for i in range(n - 1, 0, -1):
            if far if i >= half else near:
                body(me + sum(flip for bit, flip in flips.items() if i & bit))
    elif n <= 16:
        for i in range(1, n):
            if far if i >= half else near:
                body(lax.rem(me + i, n))
    else:
        low, high = 1 if near else half, n if far else half
        lax.fori_loop(low, high, lambda i, c: (body(lax.rem(me + i, n)), c)[1], 0)


def placing_of(routes, slots, copies):
    top, rows = routes.shape
    shape = (slots * copies, rows)
    line = lax.broadcasted_iota(jnp.int32, shape, 0)
    expert = line // (CAP * copies)
    slot = (line % CAP).astype(jnp.float32)
    hits = [(routes[k : k + 1, :] == expert).astype(jnp.float32) for k in range(top)]
    chosen = sum(hits[1:], hits[0])
    r = lax.broadcasted_iota(jnp.int32, (rows, rows), 0)
    c = lax.broadcasted_iota(jnp.int32, (rows, rows), 1)
    before = jnp.dot(chosen, (r < c).astype(jnp.float32), preferred_element_type=jnp.float32)
    placing = chosen * (before == slot).astype(jnp.float32)
    return placing, hits


def kernel(
    n, copies, kcuts, fcuts, dcuts,
    routes_h, weights_h, rows_h, gate_h, up_h, down_h, out_ref,
    routes_v, weights_v, rows_v, gate_v, up_v, down_v,
    packed, landed, merged, mine, theirs, hidden, begun, outbox,
    small_sem, weight_sem, send_sem, recv_sem,
    pair_send, pair_recv, back_recv,
):
    me = lax.axis_index("expert")
    partner = 1 - lax.axis_index("head")
    nk, nf, nd = len(kcuts), len(fcuts), len(dcuts)
    arrived, returned = landed.at[pl.ds(0, n)], landed.at[pl.ds(n, n)]

    small = [
        pltpu.make_async_copy(s, d, small_sem.at[i])
        for i, (s, d) in enumerate([(routes_h, routes_v), (weights_h, weights_v), (rows_h, rows_v)])
    ]
    for copy in small:
        copy.start()

    streams = []

    def stream(source, target, lines, cols):
        where = (pl.ds(*lines), pl.ds(*cols))
        streams.append(
            pltpu.make_async_copy(source.at[where], target.at[where], weight_sem.at[len(streams)])
        )
        return streams[-1]

    whole = (0, gate_v.shape[1])
    slabs = [
        [stream(gate_h, gate_v, lines, whole), stream(up_h, up_v, lines, whole)]
        for lines in kcuts
    ]
    downs = [stream(down_h, down_v, (0, down_v.shape[0]), cols) for cols in dcuts]
    streams[0].start()

    barrier = pltpu.get_barrier_semaphore()

    def greet(peer):
        pl.semaphore_signal(barrier, inc=1, device_id={"expert": peer}, device_id_type=MESH)

    each(me, n, greet)
    pl.semaphore_signal(barrier, inc=1, device_id={"head": partner}, device_id_type=MESH)
    for copy in streams[1:]:
        copy.start()

    for copy in small:
        copy.wait()
    placing, hits = placing_of(routes_v[...], FLIGHT * CAP, 1)
    picked = jnp.dot(
        placing.astype(jnp.bfloat16), rows_v[...], preferred_element_type=jnp.float32
    )
    for f in range(FLIGHT):
        packed[f] = picked[f * CAP : (f + 1) * CAP].astype(jnp.bfloat16)
    pl.semaphore_wait(barrier, n)

    for far in [True, False]:
        for k in range(nk):
            cols = pl.ds(*kcuts[k])

            def dispatch(peer, k=k, cols=cols):
                pltpu.make_async_remote_copy(
                    src_ref=packed.at[peer // copies, :, cols], dst_ref=arrived.at[me, :, cols],
                    send_sem=send_sem, recv_sem=recv_sem.at[k],
                    device_id={"expert": peer}, device_id_type=MESH,
                ).start()

            each(me, n, dispatch, far=far, near=not far)
    arrived[me] = packed[me // copies]

    if copies == 1:
        wide = placing
    else:
        wide, hits = placing_of(routes_v[...], FLIGHT * CAP, copies)
    weight = sum(
        [hits[k] * weights_v[k : k + 1, :] for k in range(1, len(hits))],
        hits[0] * weights_v[0:1, :],
    )
    spread, thirds = (wide * weight).T, []
    for _ in range(3):
        thirds.append(spread.astype(jnp.bfloat16).astype(jnp.float32))
        spread = spread - thirds[-1]
    spread = jnp.concatenate(thirds, axis=0).astype(jnp.bfloat16)

    def gather(k):
        cols = pl.ds(*kcuts[k])
        others = arrived.at[pl.ds(0, n - 1), :, cols]
        pltpu.make_async_copy(others, others, recv_sem.at[k]).wait()
        merged[:, cols] = arrived[:, :, cols].reshape(n * CAP, kcuts[k][1])

    def product(k, weights, cols):
        lines = pl.ds(*kcuts[k])
        return jnp.dot(
            merged[:, lines], weights[lines, pl.ds(*cols)], preferred_element_type=jnp.float32
        )

    pairs = [
        pltpu.make_async_remote_copy(
            src_ref=mine.at[j], dst_ref=theirs.at[j],
            send_sem=pair_send, recv_sem=pair_recv.at[j],
            device_id={"head": partner}, device_id_type=MESH,
        )
        for j in range(nf)
    ]

    def activate(j):
        pairs[j].wait_recv()
        gate = mine[j, 0] + theirs[j, 0]
        up = mine[j, 1] + theirs[j, 1]
        hidden[:, pl.ds(*fcuts[j])] = (gate / (1.0 + jnp.exp(-gate)) * up).astype(jnp.bfloat16)

    for k in range(nk - 1):
        gather(k)
        for part, weights in enumerate([gate_v, up_v]):
            slabs[k][part].wait()
            term = product(k, weights, whole)
            for j in range(nf):
                piece = term[:, fcuts[j][0] : sum(fcuts[j])]
                mine[j, part] = piece if k == 0 else mine[j, part] + piece
    gather(nk - 1)
    for part, weights in enumerate([gate_v, up_v]):
        slabs[nk - 1][part].wait()
        for j in range(nf):
            term = product(nk - 1, weights, fcuts[j])
            mine[j, part] = term if nk == 1 else mine[j, part] + term
            if part:
                pairs[j].start()
    for j in range(nf - 1):
        activate(j)

    head = fcuts[-1][0]
    early = EARLY if head else 0
    for j in range(early):
        downs[j].wait()
        cols = pl.ds(*dcuts[j])
        begun[:, cols] = jnp.dot(
            hidden[:, :head], down_v[:head, cols], preferred_element_type=jnp.float32
        )
    activate(nf - 1)

    def emit(j, part):
        cols = pl.ds(*dcuts[j])
        outbox[:, :, cols] = part.astype(jnp.bfloat16).reshape(n, CAP, dcuts[j][1])

        def give(peer):
            pltpu.make_async_remote_copy(
                src_ref=outbox.at[peer, :, cols], dst_ref=returned.at[me, :, cols],
                send_sem=send_sem, recv_sem=back_recv.at[j],
                device_id={"expert": peer}, device_id_type=MESH,
            ).start()

        each(me, n, give)

    ready = []
    for j in range(nd):
        cols = pl.ds(*dcuts[j])
        if j < early:
            part = begun[:, cols] + jnp.dot(
                hidden[:, head:], down_v[head:, cols], preferred_element_type=jnp.float32
            )
        else:
            downs[j].wait()
            part = jnp.dot(hidden[...], down_v[:, cols], preferred_element_type=jnp.float32)
        ready.append((j, part))
        while len(ready) > (1 if True else 0):
            emit(*ready.pop(0))
    for item in ready:
        emit(*item)
    returned[me] = outbox[me]

    for j in range(nd):
        cols = pl.ds(*dcuts[j])
        others = returned.at[pl.ds(0, n - 1), :, cols]
        pltpu.make_async_copy(others, others, back_recv.at[j]).wait()
        rows = returned[:, :, cols].reshape(n * CAP, dcuts[j][1])
        total = jnp.dot(spread, rows, preferred_element_type=jnp.float32)
        high, middle, low = jnp.split(total, 3, axis=0)
        out_ref[:, cols] = (high + (middle + low)).astype(out_ref.dtype)

    both = landed.at[pl.ds(0, 2 * n - 2)]
    pltpu.make_async_copy(both, both, send_sem).wait()
    pltpu.make_async_copy(mine, mine, pair_send).wait()


def per_device(moe_in, routes, gate_weights, w_gate, w_up, w_down):
    n = lax.axis_size("expert")
    copies = n // FLIGHT
    routes, gate_weights = routes.T, gate_weights.T
    rows, width = moe_in.shape
    ff = w_gate.shape[1]
    count = n * CAP
    kcuts, fcuts, dcuts = cuts_of(width, FEATURES), cuts_of(ff, GATE_COLS), cuts_of(width, DOWN_COLS)
    nk, nf, nd = len(kcuts), len(fcuts), len(dcuts)
    bf16, f32 = jnp.bfloat16, jnp.float32
    anywhere = pl.BlockSpec(memory_space=pltpu.HBM)
    dma = pltpu.SemaphoreType.DMA
    return pl.pallas_call(
        functools.partial(kernel, n, copies, kcuts, fcuts, dcuts),
        out_shape=jax.ShapeDtypeStruct((rows, width), bf16),
        in_specs=[anywhere] * 6,
        out_specs=pl.BlockSpec(memory_space=pltpu.VMEM),
        scratch_shapes=[
            pltpu.VMEM(routes.shape, routes.dtype),
            pltpu.VMEM(gate_weights.shape, gate_weights.dtype),
            pltpu.VMEM(moe_in.shape, moe_in.dtype),
            pltpu.VMEM(w_gate.shape, w_gate.dtype),
            pltpu.VMEM(w_up.shape, w_up.dtype),
            pltpu.VMEM(w_down.shape, w_down.dtype),
            pltpu.VMEM((FLIGHT, CAP, width), bf16),
            pltpu.VMEM((2 * n, CAP, width), bf16),
            pltpu.VMEM((count, width), bf16),
            pltpu.VMEM((nf, 2, count, fcuts[0][1]), f32),
            pltpu.VMEM((nf, 2, count, fcuts[0][1]), f32),
            pltpu.VMEM((count, ff), bf16),
            pltpu.VMEM((count, width), f32),
            pltpu.VMEM((n, CAP, width), bf16),
            dma((3,)), dma((2 * nk + nd,)), dma, dma((nk,)),
            dma, dma((nf,)), dma((nd,)),
        ],
        compiler_params=pltpu.CompilerParams(
            vmem_limit_bytes=50 << 20, collective_id=0, has_side_effects=True),
    )(*[pltpu.with_memory_space_constraint(v, pltpu.HBM) for v in (routes, gate_weights, moe_in)], w_gate, w_up, w_down)


def solution(mesh):
    in_specs = (
        P(("groups", "expert"), "head"),
        P(("groups", "expert"), None),
        P(("groups", "expert"), None),
        P("head", "expert"),
        P("head", "expert"),
        P("expert", "head"),
    )
    out_specs = P(("groups", "expert"), "head")
    return jax.shard_map(
        per_device, mesh=mesh, in_specs=in_specs, out_specs=out_specs, check_vma=False
    )
```
